256 devices in a mesh: trav: 8 (over z), bulk: 32 (over y, x, core).
Axes of the slice: x: 4, y: 4, z: 8, core: 2. Of those that a mesh axis runs over, the one named last changes fastest.
Arguments:
- parents: bfloat16 [49152, 1024], P(('trav', 'bulk')), may hold values from -6 to 6
- act_table: bfloat16 [128, 1024], replicated, may hold values from -5 to 5
- bucket_table: bfloat16 [8192, 1024], P('bulk'), may hold values from -5 to 5
- w_first: bfloat16 [1024, 2048], P(('trav', 'bulk')), may hold values from -0.1875 to 0.1875
- b_first: float32 [2048], replicated, may hold values from -3 to 3
- w_second: bfloat16 [2048, 2048], P(('trav', 'bulk')), may hold values from -0.1875 to 0.1875
- b_second: float32 [2048], replicated, may hold values from -3 to 3
- w_head: bfloat16 [2048, 8], replicated, may hold values from -0.1875 to 0.1875
- b_head: float32 [8], replicated, may hold values from -3 to 3
- branch_counts: int32 [49152], P(('trav', 'bulk')), may hold values from 1 to 4
- sampled_actions: int32 [49152, 4], P(('trav', 'bulk')), may hold values from 0 to 127
- bucket_owner: int32 [49152, 1], P(('trav', 'bulk')), may hold values from 0 to 31; in each aligned block of 192 rows (0 to 191, 192 to 383, ...) at most 8 rows name the same one
- bucket_row: int32 [49152], P(('trav', 'bulk')), may hold values from 0 to 255
- legal_mask: int32 [49152, 32], P(('trav', 'bulk')), may hold values 0 or 1
- ancestor: int32 [49152], P(('trav', 'bulk')), may hold values from 0 to 47
Outputs:
- strategy: float32 [49152, 32], P(('trav', 'bulk'))
- ancestor_value: float32 [12288], P(('trav', 'bulk'))
The draws below stay inside these ranges and needn't reach their ends.
Inputs may be any that keep to these rules, and one draw needn't show every extreme that they name: `bucket_owner`: in each aligned block of 192 histories (the histories of one device) no evaluator is named more than 8 times, a bound that some block reaches.
All inputs are finite; a program needn't handle non-finite values. No bound on the sum of `legal_mask` on one device may be relied on, other than what follows from the above.
Results may differ from the reference program's by a relative error of at most 0.0078.
Values may be sent and summed in bfloat16 or wider, within the bound.
A program may use at most 64 MiB of HBM per device.

```python
import math
import jax
import jax.numpy as jnp
import numpy as np
from jax import lax

F = 1024
H = 2048
ACTIONS = 8
KMAX = 4
ACT_VOCAB = 128
BUCK_DEV = 256
PAR_DEV = 192
NPAR = 49152
CAP = 8
BUCKETS = 8192
ANC_DEV = 48
ANCESTORS = 12288
N_BULK = 32


def touch_ends(array, stream_key, smallest, top_value):
    longest = array.shape.index(max(array.shape))
    spots = []
    for shift in (0, 1):
        where = [jax.random.randint(jax.random.fold_in(stream_key, axis), (), 0, length) for axis, length in enumerate(array.shape)]
        where[longest] = (where[longest] + shift) % array.shape[longest]
        spots.append(tuple(where))
    return array.at[spots[0]].set(smallest).at[spots[1]].set(top_value)


def block_levels(stream_key, shape, shards, smallest, high):
    loudness = 1.0
    for dim, blocks in shards:
        steps = jax.random.uniform(jax.random.fold_in(jax.random.fold_in(stream_key, 6), dim), (blocks,), jnp.float32, smallest / len(shards), high / len(shards))
        loudness = loudness * jnp.repeat(jnp.exp(steps), shape[dim] // blocks).reshape((-1,) + (1,) * (len(shape) - 1 - dim))
    return loudness


def deal_out(stream_key, own, number, rows, number_of, top, limit, slope):
    ranking = jax.random.permutation(stream_key, number_of)
    heavy_load, ordinary = portions_of(number_of, rows * top, limit, slope, True), portions_of(number_of, rows * top, limit, slope, False)
    places = jnp.arange(number_of)

    def named(tallies, rotation):
        used = int((tallies > 0).sum())
        fixed = max(1, used // 4)
        moved = fixed + (places - fixed + rotation * (used - fixed)) % max(1, number_of - fixed)
        return jnp.zeros((number_of,), jnp.int32).at[ranking[jnp.where(places < fixed, places, moved)]].set(jnp.asarray(tallies, jnp.int32))

    tallies = jnp.where(number % 4 == 0, named(heavy_load, number // 4), named(ordinary, number - number // 4 - 1))
    mixed = jax.random.permutation(jax.random.fold_in(own, 3), number_of)
    donor, receiver = mixed[0:number_of // 2 * 2:2], mixed[1:number_of // 2 * 2:2]
    margin = jnp.minimum(tallies[donor] - 1, limit - tallies[receiver]) // 2
    margin = jnp.where((donor == ranking[0]) | (receiver == ranking[0]) | (tallies[receiver] == 0), 0, jnp.maximum(margin, 0))
    moved = jax.random.randint(jax.random.fold_in(own, 4), (number_of // 2,), 0, 1 << 20) % (margin + 1)
    tallies = tallies.at[donor].add(-moved).at[receiver].add(moved)
    labels = jnp.searchsorted(jnp.cumsum(tallies), jnp.arange(rows * top), side="right").astype(jnp.int32)
    table = labels.reshape(top, rows).T
    table = table[jax.random.permutation(jax.random.fold_in(own, 1), rows)]
    rotation = jax.random.randint(jax.random.fold_in(own, 2), (rows, 1), 0, top)
    return jnp.take_along_axis(table, (jnp.arange(top)[None, :] + rotation) % top, axis=1)


def portions_of(number_of, total, most, slope, full):
    weights = [(1 << 20) // math.isqrt(grade ** slope) + 1 for grade in range(1, number_of + 1)]
    largest = most if full else min(most, max(-(-total // number_of), total * weights[0] // sum(weights)))
    least = 1 if total - largest >= number_of - 1 else 0
    given, surplus = [largest] + [least] * (number_of - 1), total - largest - least * (number_of - 1)
    while surplus > 0:
        free = [i for i in range(1, number_of) if given[i] < largest] or [i for i in range(1, number_of) if given[i] < most]
        pool, left = sum([weights[i] for i in free]), surplus
        for i in free:
            more = min(most - given[i], max(1, left * weights[i] // pool), surplus)
            given[i] = given[i] + more
            surplus = surplus - more
    return np.array(given)


def scatter_about(key, shape, scale, most, cuts=(), held_as=jnp.bfloat16):
    drawn = scale * jax.random.normal(key, shape, jnp.float32)
    if cuts:
        drawn = drawn * block_levels(key, shape, cuts, -0.22, 0.18)
    return jnp.clip(drawn, -most, most).astype(held_as)


def setup_inputs(seed: int = 0) -> dict:
    keys = jax.random.split(jax.random.key(seed), 16)
    parents = scatter_about(keys[0], (NPAR, F), 1.0, 6.0, ((0, 256),))
    act_table = scatter_about(keys[1], (ACT_VOCAB, F), 0.7, 5.0)
    bucket_table = scatter_about(keys[2], (BUCKETS, F), 0.7, 5.0, ((0, 32),))
    w_first = scatter_about(keys[3], (F, H), F ** -0.5, 0.1875, ((0, 256),))
    b_first = scatter_about(keys[4], (H,), 0.5, 3.0, (), jnp.float32)
    w_second = scatter_about(keys[5], (H, H), (H // 2) ** -0.5, 0.1875, ((0, 256),))
    b_second = scatter_about(keys[6], (H,), 0.5, 3.0, (), jnp.float32)
    w_head = scatter_about(keys[7], (H, ACTIONS), (H // 2) ** -0.5, 0.1875)
    b_head = scatter_about(keys[8], (ACTIONS,), 0.5, 3.0, (), jnp.float32)
    branch_counts = touch_ends(jax.random.randint(keys[9], (NPAR,), 1, KMAX + 1), jax.random.fold_in(keys[9], 1), 1, KMAX).astype(jnp.int32)
    sampled_actions = touch_ends(jax.random.randint(keys[10], (NPAR, KMAX), 0, ACT_VOCAB), jax.random.fold_in(keys[10], 1), 0, ACT_VOCAB - 1).astype(jnp.int32)
    bucket_owner_keys = jax.random.split(jax.random.fold_in(keys[11], 1), NPAR // PAR_DEV)
    bucket_owner_turns = jax.random.permutation(jax.random.fold_in(keys[11], 3), NPAR // PAR_DEV)
    bucket_owner = jax.vmap(lambda own, number: deal_out(jax.random.fold_in(keys[11], 2), own, number, PAR_DEV, N_BULK, 1, CAP, 2))(bucket_owner_keys, bucket_owner_turns).reshape((NPAR, 1))
    bucket_row = touch_ends(jax.random.randint(keys[12], (NPAR,), 0, BUCK_DEV), jax.random.fold_in(keys[12], 1), 0, BUCK_DEV - 1).astype(jnp.int32)
    legal_mask = touch_ends((jax.random.randint(keys[13], (NPAR, KMAX * ACTIONS), 0, 2) < 1).astype(jnp.int32), jax.random.fold_in(keys[13], 1), 0, 1)
    ancestor = touch_ends(jax.random.randint(keys[14], (NPAR,), 0, ANC_DEV), jax.random.fold_in(keys[14], 1), 0, ANC_DEV - 1).astype(jnp.int32)
    return {"parents": parents, "act_table": act_table, "bucket_table": bucket_table, "w_first": w_first, "b_first": b_first, "w_second": w_second, "b_second": b_second, "w_head": w_head, "b_head": b_head, "branch_counts": branch_counts, "sampled_actions": sampled_actions, "bucket_owner": bucket_owner, "bucket_row": bucket_row, "legal_mask": legal_mask, "ancestor": ancestor}


tremble = 0.05


def network(inputs, w_first, b_first, w_second, b_second, w_head, b_head):
    first = jnp.dot(inputs, w_first, preferred_element_type=jnp.float32) + b_first
    hidden_one = jnp.maximum(first, 0.0).astype(jnp.bfloat16)
    second = jnp.dot(hidden_one, w_second, preferred_element_type=jnp.float32) + b_second
    hidden_two = jnp.maximum(second, 0.0).astype(jnp.bfloat16)
    return jnp.dot(hidden_two, w_head, preferred_element_type=jnp.float32) + b_head


def reference(parents, act_table, bucket_table, w_first, b_first, w_second, b_second, w_head, b_head, branch_counts, sampled_actions, bucket_owner, bucket_row, legal_mask, ancestor):
    blocks = NPAR // PAR_DEV
    buckets_all = (bucket_owner[:, 0] * BUCK_DEV + bucket_row).astype(jnp.int32)
    first_action = (jnp.arange(ACTIONS) == 0).astype(jnp.float32)

    def one_block(index):
        begin = (index * PAR_DEV).astype(jnp.int32)
        par_rows = lax.dynamic_slice_in_dim(parents, begin, PAR_DEV, 0)
        actions = lax.dynamic_slice_in_dim(sampled_actions, begin, PAR_DEV, 0)
        buckets = lax.dynamic_slice_in_dim(buckets_all, begin, PAR_DEV, 0)
        counts = lax.dynamic_slice_in_dim(branch_counts, begin, PAR_DEV, 0)
        legal = lax.dynamic_slice_in_dim(legal_mask, begin, PAR_DEV, 0)
        act_rows = jnp.take(act_table, actions.reshape(-1), axis=0).reshape(PAR_DEV, KMAX, F)
        base = (par_rows.astype(jnp.float32)[:, None, :] + act_rows.astype(jnp.float32)).astype(jnp.bfloat16)
        base = lax.optimization_barrier(base)
        bucket_rows = jnp.take(bucket_table, buckets, axis=0)
        inputs = (base.astype(jnp.float32) + bucket_rows.astype(jnp.float32)[:, None, :]).astype(jnp.bfloat16)
        advantage = network(inputs.reshape(PAR_DEV * KMAX, F), w_first, b_first, w_second, b_second, w_head, b_head)
        advantage = advantage.reshape(PAR_DEV, KMAX, ACTIONS)
        allowed = jnp.maximum(legal.reshape(PAR_DEV, KMAX, ACTIONS).astype(jnp.float32), first_action)
        positive = allowed * (jnp.maximum(advantage, 0.0) + tremble)
        sigma = positive / jnp.sum(positive, axis=-1, keepdims=True)
        live = (jnp.arange(KMAX)[None, :] < counts[:, None]).astype(jnp.float32)
        strategy = sigma * live[:, :, None]
        branch_value = jnp.sum(sigma * advantage, axis=-1)
        history_value = jnp.sum(branch_value * live, axis=1) / counts.astype(jnp.float32)
        return strategy.reshape(PAR_DEV, KMAX * ACTIONS), history_value

    strategy, history_value = lax.map(one_block, jnp.arange(blocks, dtype=jnp.int32))
    strategy = strategy.reshape(NPAR, KMAX * ACTIONS)
    owner_block = (jnp.arange(NPAR, dtype=jnp.int32) // PAR_DEV).astype(jnp.int32)
    target = (owner_block * ANC_DEV + ancestor).astype(jnp.int32)
    ancestor_value = jax.ops.segment_sum(history_value.reshape(-1), target, num_segments=ANCESTORS)
    return strategy, ancestor_value
```

```python
import functools

import jax
import jax.numpy as jnp
from jax import lax
from jax.experimental import pallas as pl
from jax.experimental.pallas import tpu as pltpu
from jax.sharding import PartitionSpec as P

MESH = pl.DeviceIdType.MESH
NZ, NY, NX, NC = 8, 4, 4, 2
NB = NY * NX * NC
TREMBLE = 0.05
PAR, KMAX, ACTIONS, F, H, CAP, VOCAB, BUCK, ANC = 192, 4, 8, 1024, 2048, 8, 128, 256, 48
HALF = H // 2
ROWS = PAR * KMAX
STAGES = (
    (0, 0, 384, 384, 256),
    (1, 0, 128, 256, 128),
    (1, 512, 256, 128, 128),
)
COPIES = 256
bf16, f32 = jnp.bfloat16, jnp.float32


def kernel(
    parents, act, table, w1, b1, w2, b2, wht, bh, counts, acts, owner, brow, legal, anc,
    out, outa,
    w1b, w2b, w1x, xs, h1, ss, gmat, ids_s, ids_r, rows_s, rows_r, pa, pt, pr,
    ssem, rsem, isem, irsem, gsem, grsem, lsem,
):
    z = lax.axis_index("trav")
    b = lax.axis_index("bulk")
    core = lax.rem(b, 2)
    x = lax.rem(lax.div(b, 2), NX)
    y = lax.div(b, 2 * NX)
    sibling = (z, b + 1 - 2 * core)
    other = 1 - core

    def dev(zz, yy, xx):
        return (lax.rem(zz + NZ, NZ), (lax.rem(yy + NY, NY) * NX + lax.rem(xx + NX, NX)) * 2 + core)

    barrier = pltpu.get_barrier_semaphore()

    def greet(j, _):
        pl.semaphore_signal(barrier, inc=1, device_id=(z, lax.rem(b + j, NB)), device_id_type=MESH)
        return 0

    lax.fori_loop(1, NB, greet, 0)
    for dz in (1, -1):
        pl.semaphore_signal(barrier, inc=1, device_id=dev(z + dz, y, x), device_id_type=MESH)

    ss[...] = jnp.full(ss.shape, -1.0, f32)
    ss[0:4, 0:PAR] = acts[...].astype(f32)
    ss[4:5, 0:PAR] = owner[...].astype(f32)
    ss[5:6, 0:PAR] = brow[...].astype(f32)
    st = ss[...].T
    lanes = lax.broadcasted_iota(jnp.int32, (256, 128), 1).astype(f32)
    sub2 = lax.broadcasted_iota(jnp.int32, (256, 256), 0).astype(f32)
    lane2 = lax.broadcasted_iota(jnp.int32, (256, 256), 1).astype(f32)
    owner_col = st[:, 4:5]
    hits = jnp.where(owner_col == lanes, 1.0, 0.0)
    below = jnp.where(sub2 > lane2, 1.0, 0.0).astype(bf16)
    rank = jnp.dot(below, hits.astype(bf16), preferred_element_type=f32)
    slot_col = owner_col * CAP + jnp.sum(rank * hits, axis=1, keepdims=True)
    gmat[...] = jnp.where(slot_col == lane2, 1.0, 0.0).astype(bf16)[0:PAR]
    owner_row = ss[4:5, :]
    hits_t = jnp.where(owner_row == sub2[0:NB], 1.0, 0.0)
    above = jnp.where(sub2 < lane2, 1.0, 0.0).astype(bf16)
    rank_t = jnp.dot(hits_t.astype(bf16), above, preferred_element_type=f32)
    slot_row = owner_row * CAP + jnp.sum(rank_t * hits_t, axis=0, keepdims=True)
    place_t = jnp.where(slot_row == sub2, 1.0, 0.0).astype(bf16)
    row_cols = jnp.broadcast_to(st[:, 5:6], (256, 128)).astype(bf16)
    ids_s[...] = jnp.dot(place_t, row_cols, preferred_element_type=f32)

    pl.semaphore_wait(barrier, NB - 1 + 2)

    counter = [0]
    started = []

    def send(src, dst, target):
        k = counter[0]
        counter[0] += 1
        copy = pltpu.make_async_remote_copy(
            src_ref=src, dst_ref=dst, send_sem=ssem.at[k], recv_sem=rsem.at[k],
            device_id=target, device_id_type=MESH,
        )
        copy.start()
        started.append(copy)
        return copy

    mine = pl.multiple_of(core * HALF, HALF)
    theirs = pl.multiple_of(other * HALF, HALF)
    to_sib = [
        send(w1.at[:, pl.ds(theirs, HALF)], w1x, sibling),
        send(w2.at[:, pl.ds(theirs, HALF)], w2b.at[z, y, x, pl.ds(pl.multiple_of(core * 8, 8), 8), :], sibling),
    ]
    own_w2 = pltpu.make_async_copy(
        w2.at[:, pl.ds(mine, HALF)], w2b.at[z, y, x, pl.ds(pl.multiple_of(core * 8, 8), 8), :], lsem.at[0]
    )
    own_w2.start()

    def eight(ref, i):
        return ref.at[pl.ds(pl.multiple_of(i * CAP, CAP), CAP), :]

    def id_copy(j):
        peer = lax.rem(b + j, NB)
        return pltpu.make_async_remote_copy(
            src_ref=eight(ids_s, peer), dst_ref=eight(ids_r, b), send_sem=isem.at[j], recv_sem=irsem.at[j],
            device_id=(z, peer), device_id_type=MESH,
        )

    def row_copy(j):
        peer = lax.rem(b + j, NB)
        return pltpu.make_async_remote_copy(
            src_ref=eight(rows_s, peer), dst_ref=eight(rows_r, b), send_sem=gsem.at[j], recv_sem=grsem.at[j],
            device_id=(z, peer), device_id_type=MESH,
        )

    def each_peer(action):
        def step(j, _):
            action(j)
            return 0

        lax.fori_loop(1, NB, step, 0)

    each_peer(lambda j: id_copy(j).start())
    own_ids = pltpu.make_async_copy(eight(ids_s, b), eight(ids_r, b), lsem.at[1])
    own_ids.start()

    to_sib[0].wait_recv()
    w1_own = w1[:, pl.ds(mine, HALF)]
    w1_sib = w1x[...]
    first = jnp.where(core == 0, w1_own.astype(f32), w1_sib.astype(f32))
    second = jnp.where(core == 0, w1_sib.astype(f32), w1_own.astype(f32))
    w1b[z, y, x] = jnp.concatenate([first, second], axis=0).astype(bf16)
    to_sib[1].wait_recv()
    own_w2.wait()

    class Stage:
        def __init__(self, layer, col, wa, wb, wc):
            self.buf = w1b if layer == 0 else w2b
            self.cols = {"A": (col, wa), "B": (col + wa, wb), "C": (col + wa + wb, wc)}
            self.done = 0
            self.flight = []

        def at(self, part, zs, ys, xs_):
            c0, w = self.cols[part]
            return self.buf.at[zs, ys, xs_, :, pl.ds(c0, w)]

        def block(self, part, axis, index, half=None):
            one = pl.ds(index, 1)
            if axis == "z" and part == "A":
                ys = pl.ds(0, NY) if half is None else pl.ds(half * NY // 2, NY // 2)
                return self.at(part, one, ys, pl.ds(x, 1))
            if axis == "z" and part == "B":
                xr = pl.ds(0, NX) if half is None else pl.ds(half * NX // 2, NX // 2)
                return self.at(part, one, pl.ds(y, 1), xr)
            if axis == "y" and part == "C":
                xr = pl.ds(0, NX) if half is None else pl.ds(half * NX // 2, NX // 2)
                return self.at(part, pl.ds(z, 1), one, xr)
            if axis == "z" and part == "C":
                ys = pl.ds(0, NY) if half is None else pl.ds(half * NY // 2, NY // 2)
                return self.at(part, one, ys, pl.ds(0, NX))
            zs = pl.ds(0, NZ) if half is None else pl.ds(half * NZ // 2, NZ // 2)
            if axis == "x":
                return self.at(part, zs, pl.ds(0, NY), one)
            return self.at(part, zs, one, pl.ds(0, NX))

        def ring(self, part, axis, d):
            n = {"z": NZ, "y": NY, "x": NX}[axis]
            me = {"z": z, "y": y, "x": x}[axis]
            for k, sign in enumerate((1, -1)):
                half = k if d == n // 2 - 1 else None
                src = self.block(part, axis, lax.rem(me - sign * d + n, n), half)
                target = dev(
                    z + sign * (axis == "z"), y + sign * (axis == "y"), x + sign * (axis == "x")
                )
                self.flight.append(send(src, src, target))

        def wait(self):
            for copy in self.flight:
                copy.wait_recv()
            self.flight = []

        def step(self):
            k = self.done
            self.done += 1
            self.wait()
            if k == 0:
                ca, wa = self.cols["A"]
                cb, wb = self.cols["B"]
                wc = self.cols["C"][1]
                own = self.buf.at[z, y, x]
                for d in (1, 3, 2):
                    ref = own.at[:, pl.ds(ca, wa)]
                    self.flight.append(send(ref, ref, dev(z, y + d, x)))
                    ref = own.at[:, pl.ds(cb, wb + wc)]
                    self.flight.append(send(ref, ref, dev(z, y, x + d)))
            elif k < 7:
                for part, axis, d in (
                    ("A", "z", k - 1) if k < 5 else ("A", "x", k - 5),
                    ("B", "z", k - 1) if k < 5 else ("B", "y", k - 5),
                    ("C", "y", k - 1) if k < 3 else ("C", "z", k - 3),
                ):
                    self.ring(part, axis, d)

    stages = [Stage(*s) for s in STAGES]
    for s in stages:
        s.step()
    s0, s1, s2 = stages
    s0.step()

    own_ids.wait()
    each_peer(lambda j: id_copy(j).wait_recv())
    ids = ids_r[...]
    onehot = jnp.concatenate(
        [jnp.where(ids == lanes, 1.0, 0.0).astype(bf16), jnp.where(ids == lanes + 128.0, 1.0, 0.0).astype(bf16)], axis=1
    )
    rows_s[...] = jnp.dot(onehot, table[...], preferred_element_type=f32).astype(bf16)
    s0.step()
    each_peer(lambda j: row_copy(j).start())
    own_rows = pltpu.make_async_copy(eight(rows_s, b), eight(rows_r, b), lsem.at[2])
    own_rows.start()

    s1.step()
    s0.step()
    act_rows = []
    for c in range(KMAX):
        oh = jnp.where(st[0:PAR, c : c + 1] == lanes[0:PAR], 1.0, 0.0).astype(bf16)
        rows = jnp.dot(oh, act[...], preferred_element_type=f32)
        xs[core, c * PAR : (c + 1) * PAR, :] = (parents[...].astype(f32) + rows).astype(bf16)
    s0.step()
    s1.step()
    own_rows.wait()
    each_peer(lambda j: row_copy(j).wait_recv())
    placed = jnp.dot(gmat[...], rows_r[...], preferred_element_type=f32)
    for c in range(KMAX):
        base = xs[core, c * PAR : (c + 1) * PAR, :].astype(f32)
        xs[core, c * PAR : (c + 1) * PAR, :] = (base + placed).astype(bf16)
    x_copy = send(xs.at[core], xs.at[core], sibling)

    for s in (s2, s0, s1, s2, s0, s1, s0, s2, s1):
        s.step()

    RC = ROWS // 2
    w1f = w1b.reshape(F, HALF)
    w2f = w2b.reshape(H, HALF)

    def layer_one(o, r):
        def tile(n, _):
            c0 = pl.multiple_of(n * 256, 256)
            acc = jnp.dot(xs[o, r * RC : (r + 1) * RC, :], w1f[:, pl.ds(c0, 256)], preferred_element_type=f32)
            bias = b1[:, pl.ds(pl.multiple_of(mine + c0, 256), 256)]
            h1[core, o, r * RC : (r + 1) * RC, pl.ds(c0, 256)] = jnp.maximum(acc + bias, 0.0).astype(bf16)
            return 0

        lax.fori_loop(0, HALF // 256, tile, 0)
        part = h1.at[core, o, pl.ds(r * RC, RC), :]
        return send(part, part, sibling)

    h_copies = [layer_one(core, 0), layer_one(core, 1)]
    s2.step()
    s1.step()
    x_copy.wait_recv()
    h_copies += [layer_one(other, 0), layer_one(other, 1)]
    s2.step()
    s1.step()
    for copy in h_copies:
        copy.wait_recv()

    def layer_two(o, r, col0, tiles):
        def tile(n, total):
            c0 = pl.multiple_of(col0 + n * 256, 256)
            acc = jnp.dot(h1[0, o, r * RC : (r + 1) * RC, :], w2f[0:HALF, pl.ds(c0, 256)], preferred_element_type=f32)
            acc += jnp.dot(h1[1, o, r * RC : (r + 1) * RC, :], w2f[HALF:H, pl.ds(c0, 256)], preferred_element_type=f32)
            g0 = pl.multiple_of(mine + c0, 256)
            hid = jnp.maximum(acc + b2[:, pl.ds(g0, 256)], 0.0).astype(bf16)
            return total + lax.dot_general(
                hid, wht[:, pl.ds(g0, 256)], (((1,), (1,)), ((), ())), preferred_element_type=f32
            )

        return lax.fori_loop(0, tiles, tile, jnp.zeros((RC, ACTIONS), f32))

    share = jnp.where(core == 0, 1.0, 0.0)
    for i, (o, r) in enumerate(((other, 0), (other, 1), (core, 0), (core, 1))):
        pa[o, r * RC : (r + 1) * RC, :] = layer_two(o, r, 0, 2) + bh[...] * share
        if i == 1:
            s2.step()
    s2.step()

    def finish(o, r):
        total = pa[o, r * RC : (r + 1) * RC, :] + layer_two(o, r, 512, 2)
        for i in range(2):
            pt[o, r * 2 + i] = total[i * PAR : (i + 1) * PAR, :].T

    finish(other, 0)
    finish(other, 1)
    p_copy = send(pt.at[other], pr, sibling)
    finish(core, 0)
    finish(core, 1)
    p_copy.wait_recv()

    count = counts[...]
    first_action = jnp.where(lax.broadcasted_iota(jnp.int32, (ACTIONS, PAR), 0) == 0, 1.0, 0.0)
    value = jnp.zeros((1, PAR), f32)
    for c in range(KMAX):
        adv = pt[core, c] + pr[c]
        allowed = jnp.maximum(legal[c * ACTIONS : (c + 1) * ACTIONS, :].astype(f32), first_action)
        positive = allowed * (jnp.maximum(adv, 0.0) + TREMBLE)
        sigma = positive / jnp.sum(positive, axis=0, keepdims=True)
        live = jnp.where(count > c, 1.0, 0.0)
        out[c * ACTIONS : (c + 1) * ACTIONS, :] = sigma * live
        value += live * jnp.sum(sigma * adv, axis=0, keepdims=True)
    value = value / count.astype(f32)
    nodes = lax.broadcasted_iota(jnp.int32, (ANC, PAR), 0)
    sums = jnp.sum(jnp.where(nodes == anc[...], value, 0.0), axis=1, keepdims=True)
    diag = lax.broadcasted_iota(jnp.int32, (ANC, ANC), 0) == lax.broadcasted_iota(jnp.int32, (ANC, ANC), 1)
    outa[...] = jnp.sum(jnp.where(diag, sums, 0.0), axis=0, keepdims=True)

    for copy in started:
        copy.wait_send()
    each_peer(lambda j: id_copy(j).wait_send())
    each_peer(lambda j: row_copy(j).wait_send())


def body(
    parents, act_table, bucket_table, w_first, b_first, w_second, b_second, w_head, b_head,
    branch_counts, sampled_actions, bucket_owner, bucket_row, legal_mask, ancestor,
):
    row = lambda a: a.reshape(1, a.shape[0])
    vmem = pl.BlockSpec(memory_space=pltpu.VMEM)
    dma = pltpu.SemaphoreType.DMA
    out, outa = pl.pallas_call(
        kernel,
        out_shape=(jax.ShapeDtypeStruct((KMAX * ACTIONS, PAR), f32), jax.ShapeDtypeStruct((1, ANC), f32)),
        in_specs=[vmem] * 15,
        out_specs=(vmem, vmem),
        scratch_shapes=[
            pltpu.VMEM((NZ, NY, NX, 8, HALF), bf16),
            pltpu.VMEM((NZ, NY, NX, 16, HALF), bf16),
            pltpu.VMEM((4, HALF), bf16),
            pltpu.VMEM((2, ROWS, F), bf16),
            pltpu.VMEM((2, 2, ROWS, HALF), bf16),
            pltpu.VMEM((128, 256), f32),
            pltpu.VMEM((PAR, 256), bf16),
            pltpu.VMEM((256, 128), f32),
            pltpu.VMEM((256, 128), f32),
            pltpu.VMEM((256, F), bf16),
            pltpu.VMEM((256, F), bf16),
            pltpu.VMEM((2, ROWS, ACTIONS), f32),
            pltpu.VMEM((2, KMAX, ACTIONS, PAR), f32),
            pltpu.VMEM((KMAX, ACTIONS, PAR), f32),
            dma((COPIES,)),
            dma((COPIES,)),
            dma((NB,)),
            dma((NB,)),
            dma((NB,)),
            dma((NB,)),
            dma((4,)),
        ],
        compiler_params=pltpu.CompilerParams(
            collective_id=0, has_side_effects=True, vmem_limit_bytes=56 * 1024 * 1024
        ),
    )(
        parents, act_table, bucket_table, w_first, row(b_first), w_second, row(b_second), w_head.T, row(b_head),
        row(branch_counts), sampled_actions.T, bucket_owner.T, row(bucket_row), legal_mask.T, row(ancestor),
    )
    return out.T, outa.reshape(ANC)


def solution(mesh):
    rows = P(("trav", "bulk"), None)
    flat = P(("trav", "bulk"))
    return jax.shard_map(
        body,
        mesh=mesh,
        in_specs=(rows, P(), P("bulk", None), rows, P(), rows, P(), P(), P(), flat, rows, rows, flat, rows, flat),
        out_specs=(rows, flat),
        check_vma=False,
    )
```

```python
import functools

import jax
import jax.numpy as jnp
from jax import lax
from jax.experimental import pallas as pl
from jax.experimental.pallas import tpu as pltpu
from jax.sharding import PartitionSpec as P

MESH = pl.DeviceIdType.MESH
NZ, NY, NX, NC = 8, 4, 4, 2
NB = NY * NX * NC
TREMBLE = 0.05
PAR, KMAX, ACTIONS, F, H, CAP, VOCAB, BUCK, ANC = 192, 4, 8, 1024, 2048, 8, 128, 256, 48
HALF = H // 2
ROWS = PAR * KMAX
STAGES = (
    (0, 0, 384, 384, 256),
    (1, 0, 128, 128, 256),
    (1, 512, 128, 128, 256),
)
COPIES = 256
INPUTS = (
    "parents", "act", "table", "w1", "b1", "w2", "b2", "wht", "bh", "counts", "acts", "owner", "brow", "legal", "anc"
)
bf16, f32 = jnp.bfloat16, jnp.float32


def kernel(*refs):
    n_in = len(INPUTS)
    inputs, (out, outa), inside = refs[:n_in], refs[n_in : n_in + 2], refs[n_in + 2 : 2 * n_in + 2]
    body_of_kernel(inputs, inside, out, outa, *refs[2 * n_in + 2 :])


def body_of_kernel(
    inputs, inside, out, outa,
    w1b, w2b, w1x, xs, h1, ss, gmat, ids_s, ids_r, rows_s, rows_r, pa, pt, pr,
    ssem, rsem, isem, irsem, gsem, grsem, lsem, nsem,
):
    parents, act, table, w1, b1, w2, b2, wht, bh, counts, acts, owner, brow, legal, anc = inside
    loads = [pltpu.make_async_copy(src, dst, nsem.at[k]) for k, (src, dst) in enumerate(zip(inputs, inside))]
    by_name = dict(zip(INPUTS, loads))
    for name in ("w1", "w2", "acts", "owner", "brow"):
        by_name[name].start()
    z = lax.axis_index("trav")
    b = lax.axis_index("bulk")
    core = lax.rem(b, 2)
    x = lax.rem(lax.div(b, 2), NX)
    y = lax.div(b, 2 * NX)
    sibling = (z, b + 1 - 2 * core)
    other = 1 - core

    def dev(zz, yy, xx):
        return (lax.rem(zz + NZ, NZ), (lax.rem(yy + NY, NY) * NX + lax.rem(xx + NX, NX)) * 2 + core)

    barrier = pltpu.get_barrier_semaphore()

    def greet(j, _):
        pl.semaphore_signal(barrier, inc=1, device_id=(z, lax.rem(b + j, NB)), device_id_type=MESH)
        return 0

    lax.fori_loop(1, NB, greet, 0)
    for dz in range(1, NZ):
        pl.semaphore_signal(barrier, inc=1, device_id=dev(z + dz, y, x), device_id_type=MESH)

    rest = [n for n in INPUTS if n not in ("w1", "w2", "acts", "owner", "brow")]
    for name in rest:
        by_name[name].start()

    pl.semaphore_wait(barrier, NB - 1 + NZ - 1)

    counter = [0]
    started = []

    def send(src, dst, target):
        k = counter[0]
        counter[0] += 1
        copy = pltpu.make_async_remote_copy(
            src_ref=src, dst_ref=dst, send_sem=ssem.at[k], recv_sem=rsem.at[k],
            device_id=target, device_id_type=MESH,
        )
        copy.start()
        started.append(copy)
        return copy

    by_name["w1"].wait()
    by_name["w2"].wait()
    mine = pl.multiple_of(core * HALF, HALF)
    theirs = pl.multiple_of(other * HALF, HALF)
    to_sib = [
        send(w1.at[:, pl.ds(theirs, HALF)], w1x, sibling),
        send(w2.at[:, pl.ds(theirs, HALF)], w2b.at[z, y, x, pl.ds(pl.multiple_of(core * 8, 8), 8), :], sibling),
    ]
    own_w2 = pltpu.make_async_copy(
        w2.at[:, pl.ds(mine, HALF)], w2b.at[z, y, x, pl.ds(pl.multiple_of(core * 8, 8), 8), :], lsem.at[0]
    )
    own_w2.start()

    for name in ("acts", "owner", "brow"):
        by_name[name].wait()
    ss[...] = jnp.full(ss.shape, -1.0, f32)
    ss[0:4, 0:PAR] = acts[...].astype(f32)
    ss[4:5, 0:PAR] = owner[...].astype(f32)
    ss[5:6, 0:PAR] = brow[...].astype(f32)
    st = ss[...].T
    lanes = lax.broadcasted_iota(jnp.int32, (256, 128), 1).astype(f32)
    sub2 = lax.broadcasted_iota(jnp.int32, (256, 256), 0).astype(f32)
    lane2 = lax.broadcasted_iota(jnp.int32, (256, 256), 1).astype(f32)
    owner_col = st[:, 4:5]
    hits = jnp.where(owner_col == lanes, 1.0, 0.0)
    below = jnp.where(sub2 > lane2, 1.0, 0.0).astype(bf16)
    rank = jnp.dot(below, hits.astype(bf16), preferred_element_type=f32)
    slot_col = owner_col * CAP + jnp.sum(rank * hits, axis=1, keepdims=True)
    gmat[...] = jnp.where(slot_col == lane2, 1.0, 0.0).astype(bf16)[0:PAR]
    owner_row = ss[4:5, :]
    hits_t = jnp.where(owner_row == sub2[0:NB], 1.0, 0.0)
    above = jnp.where(sub2 < lane2, 1.0, 0.0).astype(bf16)
    rank_t = jnp.dot(hits_t.astype(bf16), above, preferred_element_type=f32)
    slot_row = owner_row * CAP + jnp.sum(rank_t * hits_t, axis=0, keepdims=True)
    place_t = jnp.where(slot_row == sub2, 1.0, 0.0).astype(bf16)
    row_cols = jnp.broadcast_to(st[:, 5:6], (256, 128)).astype(bf16)
    ids_s[...] = jnp.dot(place_t, row_cols, preferred_element_type=f32)

    def eight(ref, i):
        return ref.at[pl.ds(pl.multiple_of(i * CAP, CAP), CAP), :]

    def id_copy(j):
        peer = lax.rem(b + j, NB)
        return pltpu.make_async_remote_copy(
            src_ref=eight(ids_s, peer), dst_ref=eight(ids_r, b), send_sem=isem.at[j], recv_sem=irsem.at[j],
            device_id=(z, peer), device_id_type=MESH,
        )

    def row_copy(j):
        peer = lax.rem(b + j, NB)
        return pltpu.make_async_remote_copy(
            src_ref=eight(rows_s, peer), dst_ref=eight(rows_r, b), send_sem=gsem.at[j], recv_sem=grsem.at[j],
            device_id=(z, peer), device_id_type=MESH,
        )

    def each_peer(action):
        def step(j, _):
            action(j)
            return 0

        lax.fori_loop(1, NB, step, 0)

    each_peer(lambda j: id_copy(j).start())
    own_ids = pltpu.make_async_copy(eight(ids_s, b), eight(ids_r, b), lsem.at[1])
    own_ids.start()

    to_sib[0].wait_recv()
    w1_own = w1[:, pl.ds(mine, HALF)]
    w1_sib = w1x[...]
    first = jnp.where(core == 0, w1_own.astype(f32), w1_sib.astype(f32))
    second = jnp.where(core == 0, w1_sib.astype(f32), w1_own.astype(f32))
    w1b[z, y, x] = jnp.concatenate([first, second], axis=0).astype(bf16)
    to_sib[1].wait_recv()
    own_w2.wait()

    class Stage:
        def __init__(self, layer, col, wa, wb, wc):
            self.buf = w1b if layer == 0 else w2b
            self.cols = {"A": (col, wa), "B": (col + wa, wb), "C": (col + wa + wb, wc)}
            self.ab_done = self.c_done = 0
            self.flight = {"A": {}, "B": {}, "C": {}}
            self.late = {"A": [], "B": [], "C": []}

        def at(self, part, zs, ys, xs_):
            c0, w = self.cols[part]
            return self.buf.at[zs, ys, xs_, :, pl.ds(c0, w)]

        def block(self, part, index, half):
            one = pl.ds(index, 1)
            if part == "C":
                return self.at(part, one, pl.ds(half * NY // 2, NY // 2), pl.ds(0, NX))
            zs = pl.ds(half * NZ // 2, NZ // 2)
            if part == "A":
                return self.at(part, zs, pl.ds(0, NY), one)
            return self.at(part, zs, one, pl.ds(0, NX))

        def ring(self, part, d):
            n, me, axis = {"A": (NX, x, "x"), "B": (NY, y, "y"), "C": (NZ, z, "z")}[part]
            before = self.flight[part]
            self.flight[part] = {}
            for k, sign in enumerate((1, -1)):
                target = dev(z + sign * (axis == "z"), y + sign * (axis == "y"), x + sign * (axis == "x"))
                for half in (k, 1 - k) if d < n // 2 - 1 else (k,):
                    if d > 0:
                        before.pop((k, half)).wait_recv()
                    src = self.block(part, lax.rem(me - sign * d + n, n), half)
                    self.flight[part][k, half] = send(src, src, target)
            self.late[part].extend(before.values() if d > 0 else ())

        def direct(self, part, src, targets):
            for target in targets:
                self.flight[part][len(self.flight[part])] = send(src, src, target)

        def wait(self, part):
            for copy in [*self.flight[part].values(), *self.late[part]]:
                copy.wait_recv()
            self.flight[part], self.late[part] = {}, []

        def ab(self):
            k = self.ab_done
            self.ab_done += 1
            if k == 0:
                c0, c1 = self.cols["A"][0], self.cols["C"][0]
                own = self.buf.at[z, y, x, :, pl.ds(c0, c1 - c0)]
                self.direct("A", own, [dev(z + d, y, x) for d in (4, 3, 5, 2, 6, 1, 7)])
            elif k == 1:
                self.wait("A")
                every, one = pl.ds(0, NZ), pl.ds(y, 1)
                self.direct("A", self.at("A", every, one, pl.ds(x, 1)), [dev(z, y + d, x) for d in (2, 1, 3)])
                self.direct("B", self.at("B", every, one, pl.ds(x, 1)), [dev(z, y, x + d) for d in (2, 1, 3)])
            else:
                for part in "AB":
                    if k in (2, 4):
                        self.wait(part)
                    if k < 4:
                        self.ring(part, k - 2)

        def c(self):
            k = self.c_done
            self.c_done += 1
            if k == 0:
                c0, w = self.cols["C"]
                self.direct("C", self.buf.at[z, y, x, :, pl.ds(c0, w)], [dev(z, y, x + d) for d in (2, 1, 3)])
            elif k == 1:
                self.wait("C")
                block = self.at("C", pl.ds(z, 1), pl.ds(y, 1), pl.ds(0, NX))
                self.direct("C", block, [dev(z, y + d, x) for d in (2, 1, 3)])
            else:
                if k in (2, 6):
                    self.wait("C")
                if k < 6:
                    self.ring("C", k - 2)

    stages = [Stage(*s) for s in STAGES]
    s0, s1, s2 = stages

    s0.ab()
    s0.c()
    s1.c()
    s1.ab()
    s2.c()
    s2.ab()
    s0.c()
    s1.c()
    s2.c()

    for name in rest:
        by_name[name].wait()
    own_ids.wait()
    each_peer(lambda j: id_copy(j).wait_recv())
    ids = ids_r[...]
    onehot = jnp.concatenate(
        [jnp.where(ids == lanes, 1.0, 0.0).astype(bf16), jnp.where(ids == lanes + 128.0, 1.0, 0.0).astype(bf16)], axis=1
    )
    rows_s[...] = jnp.dot(onehot, table[...], preferred_element_type=f32).astype(bf16)
    each_peer(lambda j: row_copy(j).start())
    own_rows = pltpu.make_async_copy(eight(rows_s, b), eight(rows_r, b), lsem.at[2])
    own_rows.start()
    s0.c()
    s1.c()
    s0.ab()
    s1.ab()
    s2.ab()

    act_rows = []
    for c in range(KMAX):
        oh = jnp.where(st[0:PAR, c : c + 1] == lanes[0:PAR], 1.0, 0.0).astype(bf16)
        rows = jnp.dot(oh, act[...], preferred_element_type=f32)
        xs[core, c * PAR : (c + 1) * PAR, :] = (parents[...].astype(f32) + rows).astype(bf16)
    s0.c()
    s2.c()
    s1.c()
    s0.ab()
    s0.c()
    own_rows.wait()
    each_peer(lambda j: row_copy(j).wait_recv())
    placed = jnp.dot(gmat[...], rows_r[...], preferred_element_type=f32)
    for c in range(KMAX):
        base = xs[core, c * PAR : (c + 1) * PAR, :].astype(f32)
        xs[core, c * PAR : (c + 1) * PAR, :] = (base + placed).astype(bf16)
    x_copy = send(xs.at[core], xs.at[core], sibling)

    s2.c()
    s1.c()
    s0.c()
    s0.ab()
    s1.ab()
    s0.c()
    s0.ab()

    RC = ROWS // 2
    w1f = w1b.reshape(F, HALF)
    w2f = w2b.reshape(H, HALF)

    def layer_one(o, r):
        rows = slice(r * RC, (r + 1) * RC)
        for c0 in range(0, HALF, 512):
            acc = jnp.dot(xs[o, rows, :], w1f[:, c0 : c0 + 512], preferred_element_type=f32)
            bias = b1[:, pl.ds(pl.multiple_of(mine + c0, 512), 512)]
            h1[core, o, rows, c0 : c0 + 512] = jnp.maximum(acc + bias, 0.0).astype(bf16)
        part = h1.at[core, o, pl.ds(r * RC, RC), :]
        return send(part, part, sibling)

    h_copies = [layer_one(core, 0)]
    s2.c()
    s2.ab()
    s1.c()
    h_copies.append(layer_one(core, 1))
    s1.ab()
    x_copy.wait_recv()
    h_copies.append(layer_one(other, 0))
    s2.c()
    h_copies.append(layer_one(other, 1))
    s2.ab()
    s1.ab()
    s1.c()
    for copy in h_copies:
        copy.wait_recv()

    def layer_two(o, c0):
        acc = jnp.dot(h1[0, o], w2f[0:HALF, c0 : c0 + 512], preferred_element_type=f32)
        acc += jnp.dot(h1[1, o], w2f[HALF:H, c0 : c0 + 512], preferred_element_type=f32)
        g0 = pl.multiple_of(mine + c0, 512)
        hid = jnp.maximum(acc + b2[:, pl.ds(g0, 512)], 0.0).astype(bf16)
        return lax.dot_general(hid, wht[:, pl.ds(g0, 512)], (((1,), (1,)), ((), ())), preferred_element_type=f32)

    share = jnp.where(core == 0, 1.0, 0.0)
    for o in (other, core):
        pa[o] = layer_two(o, 0) + bh[...] * share
    s2.ab()
    s2.c()

    def finish(o):
        total = pa[o] + layer_two(o, 512)
        for c in range(KMAX):
            pt[o, c] = total[c * PAR : (c + 1) * PAR, :].T

    finish(other)
    p_copy = send(pt.at[other], pr, sibling)
    finish(core)
    p_copy.wait_recv()

    count = counts[...]
    first_action = jnp.where(lax.broadcasted_iota(jnp.int32, (ACTIONS, PAR), 0) == 0, 1.0, 0.0)
    value = jnp.zeros((1, PAR), f32)
    for c in range(KMAX):
        adv = pt[core, c] + pr[c]
        allowed = jnp.maximum(legal[c * ACTIONS : (c + 1) * ACTIONS, :].astype(f32), first_action)
        positive = allowed * (jnp.maximum(adv, 0.0) + TREMBLE)
        sigma = positive / jnp.sum(positive, axis=0, keepdims=True)
        live = jnp.where(count > c, 1.0, 0.0)
        out[c * ACTIONS : (c + 1) * ACTIONS, :] = sigma * live
        value += live * jnp.sum(sigma * adv, axis=0, keepdims=True)
    value = value / count.astype(f32)
    nodes = lax.broadcasted_iota(jnp.int32, (ANC, PAR), 0)
    sums = jnp.sum(jnp.where(nodes == anc[...], value, 0.0), axis=1, keepdims=True)
    diag = lax.broadcasted_iota(jnp.int32, (ANC, ANC), 0) == lax.broadcasted_iota(jnp.int32, (ANC, ANC), 1)
    outa[...] = jnp.sum(jnp.where(diag, sums, 0.0), axis=0, keepdims=True)

    for copy in started:
        copy.wait_send()
    each_peer(lambda j: id_copy(j).wait_send())
    each_peer(lambda j: row_copy(j).wait_send())


def body(
    parents, act_table, bucket_table, w_first, b_first, w_second, b_second, w_head, b_head,
    branch_counts, sampled_actions, bucket_owner, bucket_row, legal_mask, ancestor,
):
    row = lambda a: a.reshape(1, a.shape[0])
    vmem = pl.BlockSpec(memory_space=pltpu.VMEM)
    operands = (
        parents, act_table, bucket_table, w_first, row(b_first), w_second, row(b_second), w_head.T, row(b_head),
        row(branch_counts), sampled_actions.T, bucket_owner.T, row(bucket_row), legal_mask.T, row(ancestor),
    )
    dma = pltpu.SemaphoreType.DMA
    out, outa = pl.pallas_call(
        kernel,
        out_shape=(jax.ShapeDtypeStruct((KMAX * ACTIONS, PAR), f32), jax.ShapeDtypeStruct((1, ANC), f32)),
        in_specs=[pl.BlockSpec(memory_space=pl.ANY)] * len(operands),
        out_specs=(vmem, vmem),
        scratch_shapes=[pltpu.VMEM(a.shape, a.dtype) for a in operands] + [
            pltpu.VMEM((NZ, NY, NX, 8, HALF), bf16),
            pltpu.VMEM((NZ, NY, NX, 16, HALF), bf16),
            pltpu.VMEM((4, HALF), bf16),
            pltpu.VMEM((2, ROWS, F), bf16),
            pltpu.VMEM((2, 2, ROWS, HALF), bf16),
            pltpu.VMEM((128, 256), f32),
            pltpu.VMEM((PAR, 256), bf16),
            pltpu.VMEM((256, 128), f32),
            pltpu.VMEM((256, 128), f32),
            pltpu.VMEM((256, F), bf16),
            pltpu.VMEM((256, F), bf16),
            pltpu.VMEM((2, ROWS, ACTIONS), f32),
            pltpu.VMEM((2, KMAX, ACTIONS, PAR), f32),
            pltpu.VMEM((KMAX, ACTIONS, PAR), f32),
            dma((COPIES,)),
            dma((COPIES,)),
            dma((NB,)),
            dma((NB,)),
            dma((NB,)),
            dma((NB,)),
            dma((4,)),
            dma((len(operands),)),
        ],
        compiler_params=pltpu.CompilerParams(
            collective_id=0, has_side_effects=True, vmem_limit_bytes=56 * 1024 * 1024
        ),
    )(*operands)
    return out.T, outa.reshape(ANC)


def solution(mesh):
    rows = P(("trav", "bulk"), None)
    flat = P(("trav", "bulk"))
    return jax.shard_map(
        body,
        mesh=mesh,
        in_specs=(rows, P(), P("bulk", None), rows, P(), rows, P(), P(), P(), flat, rows, rows, flat, rows, flat),
        out_specs=(rows, flat),
        check_vma=False,
    )
```

```python
import functools

import jax
import jax.numpy as jnp
from jax import lax
from jax.experimental import pallas as pl
from jax.experimental.pallas import tpu as pltpu
from jax.sharding import PartitionSpec as P

MESH = pl.DeviceIdType.MESH
NZ, NY, NX, NC = 8, 4, 4, 2
NB = NY * NX * NC
TREMBLE = 0.05
PAR, KMAX, ACTIONS, F, H, CAP, VOCAB, BUCK, ANC = 192, 4, 8, 1024, 2048, 8, 128, 256, 48
HALF = H // 2
ROWS = PAR * KMAX
STAGES = (
    (0, 0, 384, 384, 256),
    (1, 0, 128, 128, 256),
    (1, 512, 256, 128, 128),
)
COPIES = 256
INPUTS = (
    "parents", "act", "table", "w1", "b1", "w2", "b2", "wht", "bh", "counts", "acts", "owner", "brow", "legal", "anc"
)
bf16, f32 = jnp.bfloat16, jnp.float32


def kernel(*refs):
    n_in = len(INPUTS)
    inputs, (out, outa), inside = refs[:n_in], refs[n_in : n_in + 2], refs[n_in + 2 : 2 * n_in + 2]
    body_of_kernel(inputs, inside, out, outa, *refs[2 * n_in + 2 :])


def body_of_kernel(
    inputs, inside, out, outa,
    w1b, w2b, w1x, xs, h1, ss, gmat, ids_s, ids_r, rows_s, rows_r, pa, pt, pr,
    ssem, rsem, isem, irsem, gsem, grsem, lsem, nsem,
):
    parents, act, table, w1, b1, w2, b2, wht, bh, counts, acts, owner, brow, legal, anc = inside
    loads = [pltpu.make_async_copy(src, dst, nsem.at[k]) for k, (src, dst) in enumerate(zip(inputs, inside))]
    by_name = dict(zip(INPUTS, loads))
    for name in ("w1", "w2", "acts", "owner", "brow"):
        by_name[name].start()
    z = lax.axis_index("trav")
    b = lax.axis_index("bulk")
    core = lax.rem(b, 2)
    x = lax.rem(lax.div(b, 2), NX)
    y = lax.div(b, 2 * NX)
    sibling = (z, b + 1 - 2 * core)
    other = 1 - core

    def dev(zz, yy, xx):
        return (lax.rem(zz + NZ, NZ), (lax.rem(yy + NY, NY) * NX + lax.rem(xx + NX, NX)) * 2 + core)

    barrier = pltpu.get_barrier_semaphore()

    def greet(j, _):
        pl.semaphore_signal(barrier, inc=1, device_id=(z, lax.rem(b + j, NB)), device_id_type=MESH)
        return 0

    lax.fori_loop(1, NB, greet, 0)
    for dz in range(1, NZ):
        pl.semaphore_signal(barrier, inc=1, device_id=dev(z + dz, y, x), device_id_type=MESH)

    rest = [n for n in INPUTS if n not in ("w1", "w2", "acts", "owner", "brow")]
    for name in rest:
        by_name[name].start()

    pl.semaphore_wait(barrier, NB - 1 + NZ - 1)

    counter = [0]
    started = []

    def send(src, dst, target):
        k = counter[0]
        counter[0] += 1
        copy = pltpu.make_async_remote_copy(
            src_ref=src, dst_ref=dst, send_sem=ssem.at[k], recv_sem=rsem.at[k],
            device_id=target, device_id_type=MESH,
        )
        copy.start()
        started.append(copy)
        return copy

    by_name["w1"].wait()
    by_name["w2"].wait()
    mine = pl.multiple_of(core * HALF, HALF)
    theirs = pl.multiple_of(other * HALF, HALF)
    to_sib = [
        send(w1.at[:, pl.ds(theirs, HALF)], w1x, sibling),
        send(w2.at[:, pl.ds(theirs, HALF)], w2b.at[z, y, x, pl.ds(pl.multiple_of(core * 8, 8), 8), :], sibling),
    ]
    own_w2 = pltpu.make_async_copy(
        w2.at[:, pl.ds(mine, HALF)], w2b.at[z, y, x, pl.ds(pl.multiple_of(core * 8, 8), 8), :], lsem.at[0]
    )
    own_w2.start()

    for name in ("acts", "owner", "brow"):
        by_name[name].wait()
    ss[...] = jnp.full(ss.shape, -1.0, f32)
    ss[0:4, 0:PAR] = acts[...].astype(f32)
    ss[4:5, 0:PAR] = owner[...].astype(f32)
    ss[5:6, 0:PAR] = brow[...].astype(f32)
    st = ss[...].T
    lanes = lax.broadcasted_iota(jnp.int32, (256, 128), 1).astype(f32)
    sub2 = lax.broadcasted_iota(jnp.int32, (256, 256), 0).astype(f32)
    lane2 = lax.broadcasted_iota(jnp.int32, (256, 256), 1).astype(f32)
    owner_col = st[:, 4:5]
    hits = jnp.where(owner_col == lanes, 1.0, 0.0)
    below = jnp.where(sub2 > lane2, 1.0, 0.0).astype(bf16)
    rank = jnp.dot(below, hits.astype(bf16), preferred_element_type=f32)
    slot_col = owner_col * CAP + jnp.sum(rank * hits, axis=1, keepdims=True)
    gmat[...] = jnp.where(slot_col == lane2, 1.0, 0.0).astype(bf16)[0:PAR]
    owner_row = ss[4:5, :]
    hits_t = jnp.where(owner_row == sub2[0:NB], 1.0, 0.0)
    above = jnp.where(sub2 < lane2, 1.0, 0.0).astype(bf16)
    rank_t = jnp.dot(hits_t.astype(bf16), above, preferred_element_type=f32)
    slot_row = owner_row * CAP + jnp.sum(rank_t * hits_t, axis=0, keepdims=True)
    place_t = jnp.where(slot_row == sub2, 1.0, 0.0).astype(bf16)
    row_cols = jnp.broadcast_to(st[:, 5:6], (256, 128)).astype(bf16)
    ids_s[...] = jnp.dot(place_t, row_cols, preferred_element_type=f32)

    def eight(ref, i):
        return ref.at[pl.ds(pl.multiple_of(i * CAP, CAP), CAP), :]

    def id_copy(j):
        peer = lax.rem(b + j, NB)
        return pltpu.make_async_remote_copy(
            src_ref=eight(ids_s, peer), dst_ref=eight(ids_r, b), send_sem=isem.at[j], recv_sem=irsem.at[j],
            device_id=(z, peer), device_id_type=MESH,
        )

    def row_copy(j):
        peer = lax.rem(b + j, NB)
        return pltpu.make_async_remote_copy(
            src_ref=eight(rows_s, peer), dst_ref=eight(rows_r, b), send_sem=gsem.at[j], recv_sem=grsem.at[j],
            device_id=(z, peer), device_id_type=MESH,
        )

    def each_peer(action):
        def step(j, _):
            action(j)
            return 0

        lax.fori_loop(1, NB, step, 0)

    each_peer(lambda j: id_copy(j).start())
    own_ids = pltpu.make_async_copy(eight(ids_s, b), eight(ids_r, b), lsem.at[1])
    own_ids.start()

    to_sib[0].wait_recv()
    w1_own = w1[:, pl.ds(mine, HALF)]
    w1_sib = w1x[...]
    first = jnp.where(core == 0, w1_own.astype(f32), w1_sib.astype(f32))
    second = jnp.where(core == 0, w1_sib.astype(f32), w1_own.astype(f32))
    w1b[z, y, x] = jnp.concatenate([first, second], axis=0).astype(bf16)
    to_sib[1].wait_recv()
    own_w2.wait()

    class Stage:
        def __init__(self, layer, col, wa, wb, wc):
            self.buf = w1b if layer == 0 else w2b
            self.cols = {"A": (col, wa), "B": (col + wa, wb), "C": (col + wa + wb, wc)}
            self.ab_done = self.c_done = 0
            self.turned = layer == 1
            self.flight = {"A": {}, "B": {}, "C": {}}
            self.late = {"A": [], "B": [], "C": []}

        def at(self, part, zs, ys, xs_):
            c0, w = self.cols[part]
            return self.buf.at[zs, ys, xs_, :, pl.ds(c0, w)]

        def block(self, part, index, half):
            one = pl.ds(index, 1)
            if part == "C":
                return self.at(part, one, pl.ds(half * NY // 2, NY // 2), pl.ds(0, NX))
            zs = pl.ds(half * NZ // 2, NZ // 2)
            if part == "A":
                return self.at(part, zs, pl.ds(0, NY), one)
            return self.at(part, zs, one, pl.ds(0, NX))

        def ring(self, part, d):
            n, me, axis = {"A": (NX, x, "x"), "B": (NY, y, "y"), "C": (NZ, z, "z")}[part]
            before = self.flight[part]
            self.flight[part] = {}
            for k, sign in enumerate((1, -1)):
                target = dev(z + sign * (axis == "z"), y + sign * (axis == "y"), x + sign * (axis == "x"))
                for half in (k, 1 - k) if d < n // 2 - 1 else (k,):
                    if d > 0:
                        before.pop((k, half)).wait_recv()
                    src = self.block(part, lax.rem(me - sign * d + n, n), half)
                    self.flight[part][k, half] = send(src, src, target)
            self.late[part].extend(before.values() if d > 0 else ())

        def direct(self, part, src, targets):
            for target in targets:
                self.flight[part][len(self.flight[part])] = send(src, src, target)

        def wait(self, part):
            for copy in [*self.flight[part].values(), *self.late[part]]:
                copy.wait_recv()
            self.flight[part], self.late[part] = {}, []

        def ab(self):
            k = self.ab_done
            self.ab_done += 1
            if k == 0:
                c0, c1 = self.cols["A"][0], self.cols["C"][0]
                own = self.buf.at[z, y, x, :, pl.ds(c0, c1 - c0)]
                self.direct("A", own, [dev(z + d, y, x) for d in (4, 3, 5, 2, 6, 1, 7)])
            elif k == 1:
                self.wait("A")
                every, one = pl.ds(0, NZ), pl.ds(y, 1)
                self.direct("A", self.at("A", every, one, pl.ds(x, 1)), [dev(z, y + d, x) for d in (2, 1, 3)])
                self.direct("B", self.at("B", every, one, pl.ds(x, 1)), [dev(z, y, x + d) for d in (2, 1, 3)])
            else:
                for part in "AB":
                    if k in (2, 4):
                        self.wait(part)
                    if k < 4:
                        self.ring(part, k - 2)

        def c(self):
            k = self.c_done
            self.c_done += 1
            if k == 0:
                c0, w = self.cols["C"]
                along = (1, 0) if self.turned else (0, 1)
                self.direct(
                    "C", self.buf.at[z, y, x, :, pl.ds(c0, w)],
                    [dev(z, y + d * along[0], x + d * along[1]) for d in (2, 1, 3)],
                )
            elif k == 1:
                self.wait("C")
                along = (0, 1) if self.turned else (1, 0)
                plane = (pl.ds(0, NY), pl.ds(x, 1)) if self.turned else (pl.ds(y, 1), pl.ds(0, NX))
                self.direct(
                    "C", self.at("C", pl.ds(z, 1), *plane),
                    [dev(z, y + d * along[0], x + d * along[1]) for d in (2, 1, 3)],
                )
            else:
                if k in (2, 6):
                    self.wait("C")
                if k < 6:
                    self.ring("C", k - 2)

    stages = [Stage(*s) for s in STAGES]
    s0, s1, s2 = stages

    s0.ab()
    s0.c()
    s1.c()
    s1.ab()
    s2.c()
    s2.ab()
    s0.c()
    s1.c()
    s2.c()

    for name in rest:
        by_name[name].wait()
    own_ids.wait()
    each_peer(lambda j: id_copy(j).wait_recv())
    ids = ids_r[...]
    onehot = jnp.concatenate(
        [jnp.where(ids == lanes, 1.0, 0.0).astype(bf16), jnp.where(ids == lanes + 128.0, 1.0, 0.0).astype(bf16)], axis=1
    )
    rows_s[...] = jnp.dot(onehot, table[...], preferred_element_type=f32).astype(bf16)
    each_peer(lambda j: row_copy(j).start())
    own_rows = pltpu.make_async_copy(eight(rows_s, b), eight(rows_r, b), lsem.at[2])
    own_rows.start()
    s0.c()
    s1.c()
    s0.ab()
    s1.ab()
    s2.ab()

    act_rows = []
    for c in range(KMAX):
        oh = jnp.where(st[0:PAR, c : c + 1] == lanes[0:PAR], 1.0, 0.0).astype(bf16)
        rows = jnp.dot(oh, act[...], preferred_element_type=f32)
        xs[core, c * PAR : (c + 1) * PAR, :] = (parents[...].astype(f32) + rows).astype(bf16)
    s0.c()
    s2.c()
    s1.c()
    s0.ab()
    s0.c()
    own_rows.wait()
    each_peer(lambda j: row_copy(j).wait_recv())
    placed = jnp.dot(gmat[...], rows_r[...], preferred_element_type=f32)
    for c in range(KMAX):
        base = xs[core, c * PAR : (c + 1) * PAR, :].astype(f32)
        xs[core, c * PAR : (c + 1) * PAR, :] = (base + placed).astype(bf16)
    x_copy = send(xs.at[core], xs.at[core], sibling)

    s2.c()
    s1.c()
    s0.c()
    s0.ab()
    s1.ab()
    s0.c()
    s0.ab()

    RC = ROWS // 2
    w1f = w1b.reshape(F, HALF)
    w2f = w2b.reshape(H, HALF)

    def layer_one(o, r):
        rows = slice(r * RC, (r + 1) * RC)
        for c0 in range(0, HALF, 512):
            acc = jnp.dot(xs[o, rows, :], w1f[:, c0 : c0 + 512], preferred_element_type=f32)
            bias = b1[:, pl.ds(pl.multiple_of(mine + c0, 512), 512)]
            h1[core, o, rows, c0 : c0 + 512] = jnp.maximum(acc + bias, 0.0).astype(bf16)
        part = h1.at[core, o, pl.ds(r * RC, RC), :]
        return send(part, part, sibling)

    h_copies = [layer_one(core, 0)]
    s2.c()
    s2.ab()
    s1.c()
    h_copies.append(layer_one(core, 1))
    s1.ab()
    x_copy.wait_recv()
    h_copies.append(layer_one(other, 0))
    s2.c()
    h_copies.append(layer_one(other, 1))
    s2.ab()
    s1.ab()
    s1.c()
    for copy in h_copies:
        copy.wait_recv()

    def layer_two(o, c0):
        acc = jnp.dot(h1[0, o], w2f[0:HALF, c0 : c0 + 512], preferred_element_type=f32)
        acc += jnp.dot(h1[1, o], w2f[HALF:H, c0 : c0 + 512], preferred_element_type=f32)
        g0 = pl.multiple_of(mine + c0, 512)
        hid = jnp.maximum(acc + b2[:, pl.ds(g0, 512)], 0.0).astype(bf16)
        return lax.dot_general(hid, wht[:, pl.ds(g0, 512)], (((1,), (1,)), ((), ())), preferred_element_type=f32)

    share = jnp.where(core == 0, 1.0, 0.0)
    for o in (other, core):
        pa[o] = layer_two(o, 0) + bh[...] * share
    s2.ab()
    s2.c()

    def finish(o):
        total = pa[o] + layer_two(o, 512)
        for c in range(KMAX):
            pt[o, c] = total[c * PAR : (c + 1) * PAR, :].T

    finish(other)
    p_copy = send(pt.at[other], pr, sibling)
    finish(core)
    p_copy.wait_recv()

    count = counts[...]
    first_action = jnp.where(lax.broadcasted_iota(jnp.int32, (ACTIONS, PAR), 0) == 0, 1.0, 0.0)
    value = jnp.zeros((1, PAR), f32)
    for c in range(KMAX):
        adv = pt[core, c] + pr[c]
        allowed = jnp.maximum(legal[c * ACTIONS : (c + 1) * ACTIONS, :].astype(f32), first_action)
        positive = allowed * (jnp.maximum(adv, 0.0) + TREMBLE)
        sigma = positive / jnp.sum(positive, axis=0, keepdims=True)
        live = jnp.where(count > c, 1.0, 0.0)
        out[c * ACTIONS : (c + 1) * ACTIONS, :] = sigma * live
        value += live * jnp.sum(sigma * adv, axis=0, keepdims=True)
    value = value / count.astype(f32)
    nodes = lax.broadcasted_iota(jnp.int32, (ANC, PAR), 0)
    sums = jnp.sum(jnp.where(nodes == anc[...], value, 0.0), axis=1, keepdims=True)
    diag = lax.broadcasted_iota(jnp.int32, (ANC, ANC), 0) == lax.broadcasted_iota(jnp.int32, (ANC, ANC), 1)
    outa[...] = jnp.sum(jnp.where(diag, sums, 0.0), axis=0, keepdims=True)

    for copy in started:
        copy.wait_send()
    each_peer(lambda j: id_copy(j).wait_send())
    each_peer(lambda j: row_copy(j).wait_send())


def body(
    parents, act_table, bucket_table, w_first, b_first, w_second, b_second, w_head, b_head,
    branch_counts, sampled_actions, bucket_owner, bucket_row, legal_mask, ancestor,
):
    row = lambda a: a.reshape(1, a.shape[0])
    vmem = pl.BlockSpec(memory_space=pltpu.VMEM)
    operands = (
        parents, act_table, bucket_table, w_first, row(b_first), w_second, row(b_second), w_head.T, row(b_head),
        row(branch_counts), sampled_actions.T, bucket_owner.T, row(bucket_row), legal_mask.T, row(ancestor),
    )
    dma = pltpu.SemaphoreType.DMA
    out, outa = pl.pallas_call(
        kernel,
        out_shape=(jax.ShapeDtypeStruct((KMAX * ACTIONS, PAR), f32), jax.ShapeDtypeStruct((1, ANC), f32)),
        in_specs=[pl.BlockSpec(memory_space=pl.ANY)] * len(operands),
        out_specs=(vmem, vmem),
        scratch_shapes=[pltpu.VMEM(a.shape, a.dtype) for a in operands] + [
            pltpu.VMEM((NZ, NY, NX, 8, HALF), bf16),
            pltpu.VMEM((NZ, NY, NX, 16, HALF), bf16),
            pltpu.VMEM((4, HALF), bf16),
            pltpu.VMEM((2, ROWS, F), bf16),
            pltpu.VMEM((2, 2, ROWS, HALF), bf16),
            pltpu.VMEM((128, 256), f32),
            pltpu.VMEM((PAR, 256), bf16),
            pltpu.VMEM((256, 128), f32),
            pltpu.VMEM((256, 128), f32),
            pltpu.VMEM((256, F), bf16),
            pltpu.VMEM((256, F), bf16),
            pltpu.VMEM((2, ROWS, ACTIONS), f32),
            pltpu.VMEM((2, KMAX, ACTIONS, PAR), f32),
            pltpu.VMEM((KMAX, ACTIONS, PAR), f32),
            dma((COPIES,)),
            dma((COPIES,)),
            dma((NB,)),
            dma((NB,)),
            dma((NB,)),
            dma((NB,)),
            dma((4,)),
            dma((len(operands),)),
        ],
        compiler_params=pltpu.CompilerParams(
            collective_id=0, has_side_effects=True, vmem_limit_bytes=56 * 1024 * 1024
        ),
    )(*operands)
    return out.T, outa.reshape(ANC)


def solution(mesh):
    rows = P(("trav", "bulk"), None)
    flat = P(("trav", "bulk"))
    return jax.shard_map(
        body,
        mesh=mesh,
        in_specs=(rows, P(), P("bulk", None), rows, P(), rows, P(), P(), P(), flat, rows, rows, flat, rows, flat),
        out_specs=(rows, flat),
        check_vma=False,
    )
```
